32 devices in a mesh: dp: 16 (over z, y, x), tensor: 2 (over core).
Axes of the slice: x: 2, y: 2, z: 4, core: 2. Of those that a mesh axis runs over, the one named last changes fastest.
Arguments:
- block_input: float32 [8192, 1024], P('dp'), may hold values from -6.1 to 6.1
- output_cotangent: float32 [8192, 1024], P('dp'), may hold values from -6 to 6
- segment_ids: int32 [16, 512], P('dp'), may hold values from 0 to 3, never falling along the last dimension, each value on 1 to 256 neighbouring positions
- qkv_weight: float32 [1024, 3, 1024], P('dp', None, 'tensor'), may hold values from -1.5 to 1.5
- proj_weight: float32 [1024, 1024], P('dp', 'tensor'), may hold values from -0.375 to 0.375
- up_weight: float32 [1024, 4096], P('dp', 'tensor'), may hold values from -0.1875 to 0.1875
- down_weight: float32 [1024, 4096], P('dp', 'tensor'), may hold values from -0.09375 to 0.09375
- norm_params: float32 [4, 1024], replicated, may hold values from -1.5 to 1.6, as said below
- qkv_moments: float32 [2, 1024, 3, 1024], P(None, 'dp', None, 'tensor'), may hold values from -4 to 4, as said below
- proj_moments: float32 [2, 1024, 1024], P(None, 'dp', 'tensor'), may hold values from -4 to 4, as said below
- up_moments: float32 [2, 1024, 4096], P(None, 'dp', 'tensor'), may hold values from -4 to 4, as said below
- down_moments: float32 [2, 1024, 4096], P(None, 'dp', 'tensor'), may hold values from -4 to 4, as said below
- norm_moments: float32 [2, 4, 1024], replicated, may hold values from -4 to 4, as said below
Outputs:
- block_output: float32 [8192, 1024], P('dp')
- input_grad: float32 [8192, 1024], P('dp')
- qkv_grad: float32 [1024, 3, 1024], P('dp', None, 'tensor')
- proj_grad: float32 [1024, 1024], P('dp', 'tensor')
- up_grad: float32 [1024, 4096], P('dp', 'tensor')
- down_grad: float32 [1024, 4096], P('dp', 'tensor')
- norm_grad: float32 [4, 1024], replicated
- qkv_new: float32 [1024, 3, 1024], P('dp', None, 'tensor')
- proj_new: float32 [1024, 1024], P('dp', 'tensor')
- up_new: float32 [1024, 4096], P('dp', 'tensor')
- down_new: float32 [1024, 4096], P('dp', 'tensor')
- norm_new: float32 [4, 1024], replicated
- qkv_moments_new: float32 [2, 1024, 3, 1024], P(None, 'dp', None, 'tensor')
- proj_moments_new: float32 [2, 1024, 1024], P(None, 'dp', 'tensor')
- up_moments_new: float32 [2, 1024, 4096], P(None, 'dp', 'tensor')
- down_moments_new: float32 [2, 1024, 4096], P(None, 'dp', 'tensor')
- norm_moments_new: float32 [2, 4, 1024], replicated
The draws below stay inside these ranges and needn't reach their ends.
Inputs may be any that keep to these rules, and one draw needn't show every extreme that they name: `segment_ids`: within each row of 512 positions the ids never fall; a document is one run of equal ids. `norm_params`: rows 0 and 2 lie in 0.4 to 1.6. `qkv_moments`: the second moments are positive. `proj_moments`: the second moments are positive. `up_moments`: the second moments are positive. `down_moments`: the second moments are positive. `norm_moments`: the second moments are positive.
All inputs are finite; a program needn't handle non-finite values.
Results may differ from the reference program's by a relative error of at most 0.0075.
The reference program's roundings to bfloat16 on the way count: a program that leaves them out, or rounds other values in their place, can miss the bound.
Values may be sent and summed in bfloat16 or wider, within the bound.
No kernel may reach another device: no remote copies, remote signals or barrier semaphores. Data moves between devices by JAX's collectives and lax.ppermute only.
A program may use at most 128 MiB of HBM per device.

```python
import math
import jax
import jax.numpy as jnp
import numpy as np
from jax import lax

D = 1024
HEADS = 16
HD = 64
FF = 4096
SEQ = 512
STEP = 2
SEQS = 16
TOKENS = 8192


def draw_block_input(key, part):
    key = jax.random.fold_in(key, 21)
    return jnp.clip(jax.random.normal(key, (TOKENS, D), jnp.float32), -6.0, 6.0)


def draw_qkv_weight(key, part):
    key = jax.random.fold_in(key, 22)
    base = jnp.clip(jax.random.normal(key, (D, 3, D), jnp.float32), -5.0, 5.0) * D ** (-0.5)
    return base


def draw_norm_params(key, part):
    key = jax.random.fold_in(key, 23)
    noise = jnp.clip(jax.random.normal(key, (4, D), jnp.float32), -3.0, 3.0)
    rows = jnp.arange(4)[:, None]
    return jnp.where(rows % 2 == 0, 1.0 + 0.2 * noise, 0.5 * noise)


def moments_draw(key, shape, marker):
    key = jax.random.fold_in(key, marker)
    first = jnp.clip(jax.random.normal(key, shape, jnp.float32), -4.0, 4.0)
    second = jnp.exp(jax.random.uniform(jax.random.fold_in(key, 5), shape, jnp.float32, -3.0, -0.7))
    return jnp.stack([first, second])


def draw_qkv_moments(key, part):
    return moments_draw(key, (D, 3, D), 11)


def draw_proj_moments(key, part):
    return moments_draw(key, (D, D), 12)


def draw_up_moments(key, part):
    return moments_draw(key, (D, FF), 13)


def draw_down_moments(key, part):
    return moments_draw(key, (D, FF), 14)


def draw_norm_moments(key, part):
    return moments_draw(key, (4, D), 15)


def levels(stream_key, shape, cuts, least, largest):
    def one(axis_at, blocks):
        steps = jax.random.uniform(jax.random.fold_in(jax.random.fold_in(stream_key, 6), axis_at), (blocks,), jnp.float32, least / len(cuts), largest / len(cuts))
        return jnp.repeat(jnp.exp(steps), shape[axis_at] // blocks).reshape((-1,) + (1,) * (len(shape) - axis_at - 1))

    loudness = one(*cuts[0])
    for cut in cuts[1:]:
        loudness = loudness * one(*cut)
    return loudness


def split_up(count, total, reach, skew):
    loads = [(1 << 20) // math.isqrt(grade ** skew) + 1 for grade in range(2, count + 1)]
    rest, counts = total - reach - (count - 1), [1] * (count - 1)
    while rest > 0:
        free = [i for i in range(count - 1) if counts[i] < reach]
        pool, left = sum([loads[i] for i in free]), rest
        for i in free:
            addition = min(reach - counts[i], max(1, left * loads[i] // pool), rest)
            counts[i] = counts[i] + addition
            rest = rest - addition
    return np.array([reach] + counts)


def ragged(key, number_of, total, most, skew):
    if number_of == 2:
        one = jax.random.randint(key, (), max(1, total - most), min(most, total - 1) + 1)
        return jnp.stack([one, total - one])
    sizes = jnp.asarray(split_up(number_of, total, most, skew), jnp.int32)
    couples = (number_of - 1) // 2
    donor, sink = sizes[1:1 + 2 * couples:2], sizes[2:2 + 2 * couples:2]
    room = jnp.minimum(donor - 1, most - sink)
    moved = jax.random.randint(jax.random.fold_in(key, 1), (couples,), 0, 1 << 20) % (room + 1)
    sizes = sizes.at[1:1 + 2 * couples:2].set(donor - moved).at[2:2 + 2 * couples:2].set(sink + moved)
    return sizes[jax.random.permutation(jax.random.fold_in(key, 2), number_of)]


def normal_values(rng, shape, width, reach, shards=(), dtype=jnp.bfloat16):
    loudness = levels(rng, shape, shards, -0.22, 0.18) if shards else 1.0
    entries = jax.random.normal(rng, shape, jnp.float32) * width * loudness
    return jnp.minimum(jnp.maximum(entries, -reach), reach).astype(dtype)


def setup_inputs(seed: int = 0) -> dict:
    splits = jax.random.split(jax.random.key(seed), 14)
    block_input = draw_block_input(jax.random.fold_in(splits[13], 71), 0)
    output_cotangent = normal_values(splits[1], (TOKENS, D), 1.0, 6.0, ((0, 16),), jnp.float32)
    segment_ids = jax.vmap(lambda own: jnp.searchsorted(jnp.cumsum(ragged(own, 4, SEQ, SEQ // 2, 1)), jnp.arange(SEQ), side="right"))(jax.random.split(splits[2], SEQS)).reshape((SEQS, SEQ)).astype(jnp.int32)
    qkv_weight = draw_qkv_weight(jax.random.fold_in(splits[13], 71), 0)
    proj_weight = normal_values(splits[4], (D, D), (D // 4) ** -0.5, 0.375, ((0, 16), (1, 2)), jnp.float32)
    up_weight = normal_values(splits[5], (D, FF), D ** -0.5, 0.1875, ((0, 16), (1, 2)), jnp.float32)
    down_weight = normal_values(splits[6], (D, FF), FF ** -0.5, 0.09375, ((0, 16), (1, 2)), jnp.float32)
    norm_params = draw_norm_params(jax.random.fold_in(splits[13], 71), 0)
    qkv_moments = draw_qkv_moments(jax.random.fold_in(splits[13], 71), 0)
    proj_moments = draw_proj_moments(jax.random.fold_in(splits[13], 71), 0)
    up_moments = draw_up_moments(jax.random.fold_in(splits[13], 71), 0)
    down_moments = draw_down_moments(jax.random.fold_in(splits[13], 71), 0)
    norm_moments = draw_norm_moments(jax.random.fold_in(splits[13], 71), 0)
    return {"block_input": block_input, "output_cotangent": output_cotangent, "segment_ids": segment_ids, "qkv_weight": qkv_weight, "proj_weight": proj_weight, "up_weight": up_weight, "down_weight": down_weight, "norm_params": norm_params, "qkv_moments": qkv_moments, "proj_moments": proj_moments, "up_moments": up_moments, "down_moments": down_moments, "norm_moments": norm_moments}


norm_eps = 1e-05
beta_one = 0.9
beta_two = 0.999
adam_eps = 1e-08
learn_rate = 0.006
decay_rate = 0.1
gelu_coef = 0.7978845608028654
masked_score = -1e+30

def round_low(values):
    return lax.optimization_barrier(values.astype(jnp.bfloat16)).astype(jnp.float32)

def layer_norm(values, gain, shift):
    center = values - lax.optimization_barrier(jnp.mean(values, axis=-1, keepdims=True))
    inv_std = lax.rsqrt(lax.optimization_barrier(jnp.mean(center * center, axis=-1, keepdims=True)) + norm_eps)
    normed = center * inv_std
    return (normed * gain + shift, normed, inv_std)

def norm_backward(grad_out, normed, inv_std, gain):
    grad_normed = grad_out * gain
    return inv_std * (grad_normed - lax.optimization_barrier(jnp.mean(grad_normed, axis=-1, keepdims=True)) - normed * lax.optimization_barrier(jnp.mean(grad_normed * normed, axis=-1, keepdims=True)))

def gelu_tanh(values):
    tangent = jnp.tanh(gelu_coef * (values + 0.044715 * values * values * values))
    return 0.5 * values * (1.0 + tangent)

def gelu_slope(values):
    tangent = jnp.tanh(gelu_coef * (values + 0.044715 * values * values * values))
    return 0.5 * (1.0 + tangent) + 0.5 * values * (1.0 - tangent * tangent) * gelu_coef * (1.0 + 3.0 * 0.044715 * values * values)

def seq_mask(segment_row):
    length = segment_row.shape[0]
    rows = lax.broadcasted_iota(jnp.int32, (length, length), 0)
    cols = lax.broadcasted_iota(jnp.int32, (length, length), 1)
    return (cols <= rows) & (segment_row[:, None] == segment_row[None, :])

def scores_of(query_vals, key_vals, segment_row, scale):
    scores = jnp.einsum('qhd,khd->hqk', query_vals.astype(jnp.float32), key_vals.astype(jnp.float32)) * scale
    return jnp.where(seq_mask(segment_row)[None], scores, masked_score)

def adamw(weight, moments, grad, decay):
    first = beta_one * moments[0] + (1.0 - beta_one) * grad
    second = beta_two * moments[1] + (1.0 - beta_two) * grad * grad
    update = first / (1.0 - beta_one ** STEP) / (jnp.sqrt(second / (1.0 - beta_two ** STEP)) + adam_eps)
    return (weight - learn_rate * (update + decay * weight), jnp.stack([first, second]))

def reference(block_input, output_cotangent, segment_ids, qkv_weight, proj_weight, up_weight, down_weight, norm_params, qkv_moments, proj_moments, up_moments, down_moments, norm_moments):
    scale = HD ** (-0.5)
    qkv_flat = qkv_weight.astype(jnp.bfloat16).reshape(D, 3 * D)
    proj_low = proj_weight.astype(jnp.bfloat16)
    up_low = up_weight.astype(jnp.bfloat16)
    down_low = down_weight.astype(jnp.bfloat16)
    gain_one, shift_one, gain_two, shift_two = (norm_params[0], norm_params[1], norm_params[2], norm_params[3])

    def per_sequence(carry, inputs):
        acc_qkv, acc_proj, acc_up, acc_down, acc_norm = carry
        rows, grad_rows, segment_row = inputs
        normed_in, unit_one, inv_one = layer_norm(rows, gain_one, shift_one)
        normed_low = normed_in.astype(jnp.bfloat16)
        projected = jnp.dot(normed_low, qkv_flat, preferred_element_type=jnp.float32).astype(jnp.bfloat16)
        projected = projected.reshape(SEQ, 3, HEADS, HD)
        query_vals, key_vals, value_vals = (projected[:, 0], projected[:, 1], projected[:, 2])
        scores = scores_of(query_vals, key_vals, segment_row, scale)
        top = lax.optimization_barrier(jnp.max(scores, axis=-1, keepdims=True))
        log_total = top + jnp.log(lax.optimization_barrier(jnp.sum(jnp.exp(scores - top), axis=-1, keepdims=True)))
        probs_low = round_low(jnp.exp(scores - log_total))
        context = jnp.einsum('hqk,khd->qhd', probs_low, value_vals.astype(jnp.float32))
        context_low = context.reshape(SEQ, D).astype(jnp.bfloat16)
        mixed = rows + jnp.dot(context_low, proj_low.T, preferred_element_type=jnp.float32)
        normed_mid, unit_two, inv_two = layer_norm(mixed, gain_two, shift_two)
        mid_low = normed_mid.astype(jnp.bfloat16)
        pre_act = jnp.dot(mid_low, up_low, preferred_element_type=jnp.float32)
        act_low = gelu_tanh(pre_act).astype(jnp.bfloat16)
        result = mixed + jnp.dot(act_low, down_low.T, preferred_element_type=jnp.float32)
        grad_low = grad_rows.astype(jnp.bfloat16)
        grad_act = jnp.dot(grad_low, down_low, preferred_element_type=jnp.float32)
        acc_down = acc_down + jnp.dot(grad_low.T, act_low, preferred_element_type=jnp.float32)
        grad_pre = (grad_act * gelu_slope(pre_act)).astype(jnp.bfloat16)
        acc_up = acc_up + jnp.dot(mid_low.T, grad_pre, preferred_element_type=jnp.float32)
        grad_mid = jnp.dot(grad_pre, up_low.T, preferred_element_type=jnp.float32)
        grad_mixed = grad_rows + norm_backward(grad_mid, unit_two, inv_two, gain_two)
        mixed_low = grad_mixed.astype(jnp.bfloat16)
        acc_proj = acc_proj + jnp.dot(mixed_low.T, context_low, preferred_element_type=jnp.float32)
        grad_context = jnp.dot(mixed_low, proj_low, preferred_element_type=jnp.float32).astype(jnp.bfloat16)
        grad_block = grad_context.reshape(SEQ, HEADS, HD).astype(jnp.float32)
        probs = jnp.exp(scores_of(query_vals, key_vals, segment_row, scale) - log_total)
        probs_back = round_low(probs)
        grad_value = jnp.einsum('hqk,qhd->khd', probs_back, grad_block)
        grad_probs = jnp.einsum('qhd,khd->hqk', grad_block, value_vals.astype(jnp.float32))
        delta = lax.optimization_barrier(jnp.sum(probs * grad_probs, axis=-1, keepdims=True))
        grad_scores = round_low(probs * (grad_probs - delta) * scale)
        grad_query = jnp.einsum('hqk,khd->qhd', grad_scores, key_vals.astype(jnp.float32))
        grad_key = jnp.einsum('hqk,qhd->khd', grad_scores, query_vals.astype(jnp.float32))
        grad_flat = jnp.stack([grad_query, grad_key, grad_value], axis=1).reshape(SEQ, 3 * D).astype(jnp.bfloat16)
        acc_qkv = acc_qkv + jnp.dot(normed_low.T, grad_flat, preferred_element_type=jnp.float32).reshape(D, 3, D)
        grad_normed = jnp.dot(grad_flat, qkv_flat.T, preferred_element_type=jnp.float32)
        grad_input = grad_mixed + norm_backward(grad_normed, unit_one, inv_one, gain_one)
        acc_norm = acc_norm + jnp.stack([lax.optimization_barrier(jnp.sum(grad_normed * unit_one, axis=0)), lax.optimization_barrier(jnp.sum(grad_normed, axis=0)), lax.optimization_barrier(jnp.sum(grad_mid * unit_two, axis=0)), lax.optimization_barrier(jnp.sum(grad_mid, axis=0))])
        return ((acc_qkv, acc_proj, acc_up, acc_down, acc_norm), (result, grad_input))
    start = (jnp.zeros((D, 3, D), jnp.float32), jnp.zeros((D, D), jnp.float32), jnp.zeros((D, FF), jnp.float32), jnp.zeros((D, FF), jnp.float32), jnp.zeros((4, D), jnp.float32))
    inputs = (block_input.reshape(SEQS, SEQ, D), output_cotangent.reshape(SEQS, SEQ, D), segment_ids)
    totals, outputs = lax.scan(per_sequence, start, inputs)
    qkv_grad, proj_grad, up_grad, down_grad, norm_grad = totals
    block_output = outputs[0].reshape(TOKENS, D)
    input_grad = outputs[1].reshape(TOKENS, D)
    qkv_new, qkv_moments_new = adamw(qkv_weight, qkv_moments, qkv_grad, decay_rate)
    proj_new, proj_moments_new = adamw(proj_weight, proj_moments, proj_grad, decay_rate)
    up_new, up_moments_new = adamw(up_weight, up_moments, up_grad, decay_rate)
    down_new, down_moments_new = adamw(down_weight, down_moments, down_grad, decay_rate)
    norm_new, norm_moments_new = adamw(norm_params, norm_moments, norm_grad, 0.0)
    return (block_output, input_grad, qkv_grad, proj_grad, up_grad, down_grad, norm_grad, qkv_new, proj_new, up_new, down_new, norm_new, qkv_moments_new, proj_moments_new, up_moments_new, down_moments_new, norm_moments_new)
```

```python
import jax
import jax.numpy as jnp
from jax import lax
from jax.sharding import PartitionSpec as P

HEADS = 16
HD = 64
SEQ = 512
STEP = 2


norm_eps = 1e-05
beta_one = 0.9
beta_two = 0.999
adam_eps = 1e-08
learn_rate = 0.006
decay_rate = 0.1
gelu_coef = 0.7978845608028654
masked_score = -1e30


def layer_norm(values, gain, shift):
    center = values - jnp.mean(values, axis=-1, keepdims=True)
    inv_std = lax.rsqrt(jnp.mean(center * center, axis=-1, keepdims=True) + norm_eps)
    normed = center * inv_std
    return (normed * gain + shift, normed, inv_std)


def norm_backward(grad_out, normed, inv_std, gain):
    grad_normed = grad_out * gain
    return inv_std * (
        grad_normed
        - jnp.mean(grad_normed, axis=-1, keepdims=True)
        - normed * jnp.mean(grad_normed * normed, axis=-1, keepdims=True)
    )


def gelu_tanh(values):
    tangent = jnp.tanh(gelu_coef * (values + 0.044715 * values * values * values))
    return 0.5 * values * (1.0 + tangent)


def gelu_slope(values):
    tangent = jnp.tanh(gelu_coef * (values + 0.044715 * values * values * values))
    return 0.5 * (1.0 + tangent) + 0.5 * values * (1.0 - tangent * tangent) * gelu_coef * (
        1.0 + 3.0 * 0.044715 * values * values
    )


def seq_mask(segment_row):
    length = segment_row.shape[0]
    rows = lax.broadcasted_iota(jnp.int32, (length, length), 0)
    cols = lax.broadcasted_iota(jnp.int32, (length, length), 1)
    return (cols <= rows) & (segment_row[:, None] == segment_row[None, :])


def adamw(weight, moments, grad, decay):
    first = beta_one * moments[0] + (1.0 - beta_one) * grad
    second = beta_two * moments[1] + (1.0 - beta_two) * grad * grad
    update = first / (1.0 - beta_one**STEP) / (jnp.sqrt(second / (1.0 - beta_two**STEP)) + adam_eps)
    return (weight - learn_rate * (update + decay * weight), jnp.stack([first, second]))


def bit_groups(count):
    bits = count.bit_length() - 1
    x_bits = bits // 3
    y_bits = (bits - x_bits) // 2
    xs = list(range(x_bits - 1, -1, -1))
    ys = list(range(x_bits + y_bits - 1, x_bits - 1, -1))
    zs = list(range(bits - 1, x_bits + y_bits - 1, -1))
    return (zs, ys, xs)


def flip(count, bit):
    return [(i, i ^ (1 << bit)) for i in range(count)]


def gather_stage(block, have, bit, count, me):
    rows, cols = block.shape
    other = lax.ppermute(block, "dp", flip(count, bit))
    outer = 1 << sum(h > bit for h in have)
    upper = ((me >> bit) & 1) == 1
    mine = block.reshape(outer, 1, rows // outer, cols)
    theirs = other.reshape(outer, 1, rows // outer, cols)
    both = jnp.concatenate(
        [jnp.where(upper, theirs, mine), jnp.where(upper, mine, theirs)], axis=1
    )
    return (both.reshape(2 * rows, cols), have + [bit])


def gather_rows(block, order, count, me):
    have = []
    for bit in order:
        block, have = gather_stage(block, have, bit, count, me)
    return block


def scatter_stage(block, left, bit, count, me):
    rows, cols = block.shape
    outer = 1 << sum(h > bit for h in left)
    halves = block.reshape(outer, 2, rows // outer // 2, cols)
    upper = ((me >> bit) & 1) == 1
    send = jnp.where(upper, halves[:, 0], halves[:, 1]).astype(jnp.bfloat16)
    keep = jnp.where(upper, halves[:, 1], halves[:, 0]).reshape(rows // 2, cols)
    received = lax.ppermute(send.reshape(rows // 2, cols), "dp", flip(count, bit))
    return (keep + received.astype(jnp.float32), [h for h in left if h != bit])


def scatter_rows(block, order, count, me):
    left = list(order)
    for bit in order:
        block, left = scatter_stage(block, left, bit, count, me)
    return block


def gather_weight(block, orders, count, me):
    parts = len(orders)
    width = block.shape[1] // parts
    return jnp.concatenate(
        [
            gather_rows(block[:, i * width : (i + 1) * width], order, count, me)
            for i, order in enumerate(orders)
        ],
        axis=1,
    )


def scatter_grad(block, orders, count, me):
    parts = len(orders)
    width = block.shape[1] // parts
    return jnp.concatenate(
        [
            scatter_rows(block[:, i * width : (i + 1) * width], order[::-1], count, me)
            for i, order in enumerate(orders)
        ],
        axis=1,
    )


def sum_axis(values, axis):
    count = lax.axis_size(axis)
    for bit in range(count.bit_length() - 1):
        values = values + lax.ppermute(values, axis, flip(count, bit))
    return values


def shards(
    block_input,
    output_cotangent,
    segment_ids,
    qkv_weight,
    proj_weight,
    up_weight,
    down_weight,
    norm_params,
    qkv_moments,
    proj_moments,
    up_moments,
    down_moments,
    norm_moments,
):
    tensor_count = lax.axis_size("tensor")
    local_heads = HEADS // tensor_count
    token_count = block_input.shape[0]
    seq_count = token_count // SEQ
    scale = HD ** (-0.5)
    dp_count = lax.axis_size("dp")
    me = lax.axis_index("dp")
    zs, ys, xs = bit_groups(dp_count)
    late_z = (xs + zs + ys, ys + zs + xs)
    early_z = (zs + xs + ys, zs + ys + xs)
    low = jnp.bfloat16
    qkv_flat = gather_weight(
        qkv_weight.astype(low).reshape(qkv_weight.shape[0], -1), early_z, dp_count, me
    )
    proj_full = gather_weight(proj_weight.astype(low), early_z, dp_count, me)
    up_full = gather_weight(up_weight.astype(low), late_z, dp_count, me)
    down_full = gather_weight(down_weight.astype(low), late_z, dp_count, me)
    gain_one, shift_one, gain_two, shift_two = (
        norm_params[0],
        norm_params[1],
        norm_params[2],
        norm_params[3],
    )
    normed_in, unit_one, inv_one = layer_norm(block_input, gain_one, shift_one)
    normed_low = normed_in.astype(jnp.bfloat16)
    projected = jnp.dot(normed_low, qkv_flat, preferred_element_type=jnp.float32).astype(
        jnp.bfloat16
    )
    per_seq = projected.reshape(seq_count, SEQ, 3, local_heads, HD)

    def scores_of(query_vals, key_vals, segment_row):
        scores = (
            jnp.einsum("qhd,khd->hqk", query_vals, key_vals, preferred_element_type=jnp.float32)
            * scale
        )
        return jnp.where(seq_mask(segment_row)[None], scores, masked_score)

    def attend(item):
        block, segment_row = item
        scores = scores_of(block[:, 0], block[:, 1], segment_row)
        top = jnp.max(scores, axis=-1, keepdims=True)
        log_total = top + jnp.log(jnp.sum(jnp.exp(scores - top), axis=-1, keepdims=True))
        probs = jnp.exp(scores - log_total).astype(jnp.bfloat16)
        context = jnp.einsum("hqk,khd->qhd", probs, block[:, 2], preferred_element_type=jnp.float32)
        return (context.astype(jnp.bfloat16), log_total)

    context_low, log_totals = lax.map(attend, (per_seq, segment_ids))
    context_flat = context_low.reshape(token_count, -1)
    attn_part = jnp.einsum("tc,ec->te", context_flat, proj_full, preferred_element_type=jnp.float32)
    mixed = block_input + sum_axis(attn_part, "tensor")
    normed_mid, unit_two, inv_two = layer_norm(mixed, gain_two, shift_two)
    mid_low = normed_mid.astype(jnp.bfloat16)
    pre_act = jnp.dot(mid_low, up_full, preferred_element_type=jnp.float32)
    act_low = gelu_tanh(pre_act).astype(jnp.bfloat16)
    mlp_part = jnp.einsum("tf,ef->te", act_low, down_full, preferred_element_type=jnp.float32)
    mlp_low = mlp_part.astype(low)
    tensor_flip = flip(tensor_count, 0)
    mlp_other = lax.ppermute(mlp_low, "tensor", tensor_flip)
    block_output = mixed + (mlp_low.astype(jnp.float32) + mlp_other.astype(jnp.float32))
    grad_low = output_cotangent.astype(jnp.bfloat16)
    grad_act = jnp.dot(grad_low, down_full, preferred_element_type=jnp.float32)
    grad_pre = (grad_act * gelu_slope(pre_act)).astype(jnp.bfloat16)
    mid_part = jnp.einsum("tf,df->td", grad_pre, up_full, preferred_element_type=jnp.float32)
    grad_mid = sum_axis(mid_part, "tensor")
    grad_mixed = output_cotangent + norm_backward(grad_mid, unit_two, inv_two, gain_two)
    mixed_low = grad_mixed.astype(jnp.bfloat16)
    grad_context = jnp.dot(mixed_low, proj_full, preferred_element_type=jnp.float32).astype(
        jnp.bfloat16
    )

    def attend_back(item):
        block, segment_row, log_total, grad_block = item
        query_vals, key_vals, value_vals = (block[:, 0], block[:, 1], block[:, 2])
        probs = jnp.exp(scores_of(query_vals, key_vals, segment_row) - log_total)
        probs_low = probs.astype(jnp.bfloat16)
        grad_value = jnp.einsum(
            "hqk,qhd->khd", probs_low, grad_block, preferred_element_type=jnp.float32
        )
        grad_probs = jnp.einsum(
            "qhd,khd->hqk", grad_block, value_vals, preferred_element_type=jnp.float32
        )
        delta = jnp.sum(probs * grad_probs, axis=-1, keepdims=True)
        grad_scores = (probs * (grad_probs - delta) * scale).astype(jnp.bfloat16)
        grad_query = jnp.einsum(
            "hqk,khd->qhd", grad_scores, key_vals, preferred_element_type=jnp.float32
        )
        grad_key = jnp.einsum(
            "hqk,qhd->khd", grad_scores, query_vals, preferred_element_type=jnp.float32
        )
        return jnp.stack([grad_query, grad_key, grad_value], axis=1).astype(jnp.bfloat16)

    grad_blocks = lax.map(
        attend_back,
        (per_seq, segment_ids, log_totals, grad_context.reshape(seq_count, SEQ, local_heads, HD)),
    )
    grad_flat = grad_blocks.reshape(token_count, -1)
    normed_part = jnp.einsum("tc,dc->td", grad_flat, qkv_flat, preferred_element_type=jnp.float32)
    grad_normed = sum_axis(normed_part, "tensor")
    input_grad = grad_mixed + norm_backward(grad_normed, unit_one, inv_one, gain_one)
    qkv_local = jnp.einsum(
        "td,tc->dc", normed_low, grad_flat, preferred_element_type=jnp.float32
    )
    proj_local = jnp.einsum(
        "te,tc->ec", mixed_low, context_flat, preferred_element_type=jnp.float32
    )
    down_local = jnp.einsum("te,tf->ef", grad_low, act_low, preferred_element_type=jnp.float32)
    up_local = jnp.einsum("td,tf->df", mid_low, grad_pre, preferred_element_type=jnp.float32)
    down_grad = scatter_grad(down_local, late_z, dp_count, me)
    up_grad = scatter_grad(up_local, late_z, dp_count, me)
    proj_grad = scatter_grad(proj_local, early_z, dp_count, me)
    qkv_grad = scatter_grad(qkv_local, early_z, dp_count, me).reshape(qkv_weight.shape)
    share = token_count // tensor_count
    start = lax.axis_index("tensor") * share
    grad_one = lax.dynamic_slice_in_dim(grad_normed, start, share, 0)
    unit_first = lax.dynamic_slice_in_dim(unit_one, start, share, 0)
    grad_two = lax.dynamic_slice_in_dim(grad_mid, start, share, 0)
    unit_second = lax.dynamic_slice_in_dim(unit_two, start, share, 0)
    norm_grad = jnp.stack(
        [
            jnp.sum(grad_one * unit_first, axis=0),
            jnp.sum(grad_one, axis=0),
            jnp.sum(grad_two * unit_second, axis=0),
            jnp.sum(grad_two, axis=0),
        ]
    )
    norm_grad = sum_axis(sum_axis(norm_grad, "tensor"), "dp")
    qkv_new, qkv_moments_new = adamw(qkv_weight, qkv_moments, qkv_grad, decay_rate)
    proj_new, proj_moments_new = adamw(proj_weight, proj_moments, proj_grad, decay_rate)
    up_new, up_moments_new = adamw(up_weight, up_moments, up_grad, decay_rate)
    down_new, down_moments_new = adamw(down_weight, down_moments, down_grad, decay_rate)
    norm_new, norm_moments_new = adamw(norm_params, norm_moments, norm_grad, 0.0)
    return (
        block_output,
        input_grad,
        qkv_grad,
        proj_grad,
        up_grad,
        down_grad,
        norm_grad,
        qkv_new,
        proj_new,
        up_new,
        down_new,
        norm_new,
        qkv_moments_new,
        proj_moments_new,
        up_moments_new,
        down_moments_new,
        norm_moments_new,
    )


def solution(mesh):
    in_specs = (
        P("dp", None),
        P("dp", None),
        P("dp", None),
        P("dp", None, "tensor"),
        P("dp", "tensor"),
        P("dp", "tensor"),
        P("dp", "tensor"),
        P(),
        P(None, "dp", None, "tensor"),
        P(None, "dp", "tensor"),
        P(None, "dp", "tensor"),
        P(None, "dp", "tensor"),
        P(),
    )
    out_specs = (
        P("dp", None),
        P("dp", None),
        P("dp", None, "tensor"),
        P("dp", "tensor"),
        P("dp", "tensor"),
        P("dp", "tensor"),
        P(),
        P("dp", None, "tensor"),
        P("dp", "tensor"),
        P("dp", "tensor"),
        P("dp", "tensor"),
        P(),
        P(None, "dp", None, "tensor"),
        P(None, "dp", "tensor"),
        P(None, "dp", "tensor"),
        P(None, "dp", "tensor"),
        P(),
    )
    return jax.shard_map(shards, mesh=mesh, in_specs=in_specs, out_specs=out_specs, check_vma=False)
```

```python
import jax
import jax.numpy as jnp
from jax import lax
from jax.experimental import pallas as pl
from jax.experimental.pallas import tpu as pltpu
from jax.sharding import PartitionSpec as P

DP = "dp"
TP = "tensor"
HEADS = 16
HD = 64
SEQ = 512
STEP = 2


norm_eps = 1e-05
beta_one = 0.9
beta_two = 0.999
adam_eps = 1e-08
learn_rate = 0.006
decay_rate = 0.1
gelu_coef = 0.7978845608028654
masked_score = -1e30


def layer_norm(values, gain, shift):
    center = values - jnp.mean(values, axis=-1, keepdims=True)
    inv_std = lax.rsqrt(jnp.mean(center * center, axis=-1, keepdims=True) + norm_eps)
    normed = center * inv_std
    return (normed * gain + shift, normed, inv_std)


def norm_backward(grad_out, normed, inv_std, gain):
    grad_normed = grad_out * gain
    return inv_std * (
        grad_normed
        - jnp.mean(grad_normed, axis=-1, keepdims=True)
        - normed * jnp.mean(grad_normed * normed, axis=-1, keepdims=True)
    )


def gelu_tanh(values):
    tangent = jnp.tanh(gelu_coef * (values + 0.044715 * values * values * values))
    return 0.5 * values * (1.0 + tangent)


def gelu_slope(values):
    tangent = jnp.tanh(gelu_coef * (values + 0.044715 * values * values * values))
    return 0.5 * (1.0 + tangent) + 0.5 * values * (1.0 - tangent * tangent) * gelu_coef * (
        1.0 + 3.0 * 0.044715 * values * values
    )


def seq_mask(segment_row):
    length = segment_row.shape[0]
    rows = lax.broadcasted_iota(jnp.int32, (length, length), 0)
    cols = lax.broadcasted_iota(jnp.int32, (length, length), 1)
    return (cols <= rows) & (segment_row[:, None] == segment_row[None, :])


def adamw(weight, moments, grad, decay):
    weight, grad = lax.optimization_barrier((weight, grad))
    first = beta_one * moments[0] + (1.0 - beta_one) * grad
    second = beta_two * moments[1] + (1.0 - beta_two) * grad * grad
    scaled = jnp.sqrt(second / (1.0 - beta_two**STEP)) + adam_eps
    update = first / (1.0 - beta_one**STEP) / scaled
    return (
        weight - learn_rate * (update + decay * weight),
        jnp.stack([first, second]),
    )


def bit_groups(count):
    bits = count.bit_length() - 1
    x_bits = bits // 3
    y_bits = (bits - x_bits) // 2
    xs = list(range(x_bits - 1, -1, -1))
    ys = list(range(x_bits + y_bits - 1, x_bits - 1, -1))
    zs = list(range(bits - 1, x_bits + y_bits - 1, -1))
    return (zs, ys, xs)


def flip(count, bit):
    return [(i, i ^ (1 << bit)) for i in range(count)]


def exchange(values, axis, bit):
    return lax.ppermute(values, axis, flip(lax.axis_size(axis), bit))


def gather_stage(block, have, bit, ring):
    _, me = ring
    rows, cols = block.shape
    other = exchange(block, DP, bit)
    outer = 1 << sum(h > bit for h in have)
    upper = ((me >> bit) & 1) == 1
    mine = block.reshape(outer, 1, rows // outer, cols)
    theirs = other.reshape(outer, 1, rows // outer, cols)
    both = jnp.concatenate([jnp.where(upper, theirs, mine), jnp.where(upper, mine, theirs)], axis=1)
    return (both.reshape(2 * rows, cols), have + [bit])


def gather_bits(block, have, order, ring):
    for bit in order:
        block, have = gather_stage(block, have, bit, ring)
    return (block, have)


def own_ring(ring):
    return (ring[0], lax.optimization_barrier(ring[1]))


def gather_weight(block, late, ring):
    ring = own_ring(ring)
    zs, ys, xs = bit_groups(ring[0])
    half = block.shape[1] // 2
    firsts, seconds = (xs, ys) if late else ([], [])
    left, left_have = gather_bits(block[:, :half], [], firsts, ring)
    right, right_have = gather_bits(block[:, half:], [], seconds, ring)
    both = jnp.concatenate([left, right], axis=1)
    both, _ = gather_bits(both, [], zs, ring)
    left, _ = gather_bits(both[:, :half], left_have + zs, ys if late else xs + ys, ring)
    right, _ = gather_bits(both[:, half:], right_have + zs, xs if late else ys + xs, ring)
    return jnp.concatenate([left, right], axis=1)


def scatter_stage(block, left, bit, ring):
    _, me = ring
    rows, cols = block.shape
    outer = 1 << sum(h > bit for h in left)
    halves = block.reshape(outer, 2, rows // outer // 2, cols)
    mine = (me >> bit) & 1
    send = lax.dynamic_index_in_dim(halves, 1 - mine, 1, keepdims=False).astype(jnp.bfloat16)
    received = exchange(send.reshape(rows // 2, cols), DP, bit)
    keep = lax.dynamic_index_in_dim(halves, mine, 1, keepdims=False)
    total = keep + received.reshape(keep.shape).astype(jnp.float32)
    return (total.reshape(rows // 2, cols), [h for h in left if h != bit])


def scatter_bits(block, left, order, ring):
    for bit in order:
        block, left = scatter_stage(block, left, bit, ring)
    return (block, left)


def scatter_grad(left, right, late, ring):
    ring = own_ring(ring)
    zs, ys, xs = bit_groups(ring[0])
    every = zs + ys + xs
    half = left.shape[1]
    x_up, y_up, z_up = (xs[::-1], ys[::-1], zs[::-1])
    left, left_rest = scatter_bits(left, every, y_up if late else y_up + x_up, ring)
    right, _ = scatter_bits(right, every, x_up if late else x_up + y_up, ring)
    both, _ = scatter_bits(jnp.concatenate([left, right], axis=1), left_rest, z_up, ring)
    lasts, seconds = (x_up, y_up) if late else ([], [])
    left, _ = scatter_bits(both[:, :half], lasts, lasts, ring)
    right, _ = scatter_bits(both[:, half:], seconds, seconds, ring)
    return jnp.concatenate([left, right], axis=1)


def sum_axis(values, axis):
    zs, ys, xs = bit_groups(lax.axis_size(axis))
    for bit in xs[::-1] + ys[::-1] + zs[::-1]:
        other = exchange(values, axis, bit)
        values = values + other
    return values


def attend_back_kernel(proj_ref, grad_ref, total_ref, row_ref, col_ref, out_ref, bias_ref):
    width = grad_ref.shape[1]
    length = grad_ref.shape[0]
    chunk = length // 2
    lanes = 2 * HD
    keys = lax.broadcasted_iota(jnp.int32, (length, length), 0)
    queries = lax.broadcasted_iota(jnp.int32, (length, length), 1)
    allowed = (keys <= queries) & (col_ref[0] == row_ref[0])
    bias_ref[...] = jnp.where(allowed, 0.0, masked_score)
    lane = lax.broadcasted_iota(jnp.int32, (1, lanes), 1)

    def product(left, right, dims):
        return lax.dot_general(left, right, (dims, ((), ())), preferred_element_type=jnp.float32)

    def pair(index, carry):
        at = pl.multiple_of(index * lanes, lanes)
        key = proj_ref[:, pl.ds(width + at, lanes)]
        value = proj_ref[:, pl.ds(2 * width + at, lanes)]
        grad_key = [jnp.zeros((chunk, lanes), jnp.float32) for _ in range(2)]
        grad_value = [jnp.zeros((chunk, lanes), jnp.float32) for _ in range(2)]
        for part in range(2):
            rows = slice(part * chunk, (part + 1) * chunk)
            reach = (part + 1) * chunk
            query = proj_ref[rows, pl.ds(at, lanes)] * jnp.bfloat16(HD ** (-0.5))
            grad = grad_ref[rows, pl.ds(at, lanes)]
            grad_query = jnp.zeros((chunk, lanes), jnp.float32)
            for side in range(2):
                mine = (lane >= side * HD) & (lane < (side + 1) * HD)
                query_own = jnp.where(mine, query, jnp.zeros_like(query))
                grad_own = jnp.where(mine, grad, jnp.zeros_like(grad))
                key_own = jnp.where(mine, key[:reach], jnp.zeros_like(key[:reach]))
                total = total_ref[0, pl.ds(2 * index + side, 1), rows]
                scores = product(key[:reach], query_own, ((1,), (1,)))
                probs = jnp.exp(scores - total + bias_ref[:reach, rows])
                grad_probs = product(value[:reach], grad_own, ((1,), (1,)))
                delta = jnp.sum(probs * grad_probs, axis=0, keepdims=True)
                grad_scores = (probs * (grad_probs - delta)).astype(jnp.bfloat16)
                probs_low = probs.astype(jnp.bfloat16)
                value_part = product(probs_low, grad_own, ((1,), (0,)))
                key_part = product(grad_scores, query_own, ((1,), (0,)))
                for block in range(part + 1):
                    own = slice(block * chunk, (block + 1) * chunk)
                    grad_value[block] = grad_value[block] + value_part[own]
                    grad_key[block] = grad_key[block] + key_part[own]
                grad_query = grad_query + product(grad_scores, key_own, ((0,), (0,)))
            out_ref[rows, pl.ds(at, lanes)] = (grad_query * HD ** (-0.5)).astype(jnp.bfloat16)
        for block in range(2):
            own = slice(block * chunk, (block + 1) * chunk)
            out_ref[own, pl.ds(width + at, lanes)] = grad_key[block].astype(jnp.bfloat16)
            out_ref[own, pl.ds(2 * width + at, lanes)] = grad_value[block].astype(jnp.bfloat16)
        return carry

    lax.fori_loop(0, width // lanes, pair, 0)


def attend_back(projected, grad_context, log_totals, segment_ids):
    seq_count, length = segment_ids.shape
    heads = log_totals.shape[1]
    return pl.pallas_call(
        attend_back_kernel,
        grid=(seq_count,),
        in_specs=[
            pl.BlockSpec((length, projected.shape[1]), lambda i: (i, 0)),
            pl.BlockSpec((length, grad_context.shape[1]), lambda i: (i, 0)),
            pl.BlockSpec((1, heads, length), lambda i: (i, 0, 0)),
            pl.BlockSpec((1, 1, length), lambda i: (i, 0, 0)),
            pl.BlockSpec((1, length, 1), lambda i: (i, 0, 0)),
        ],
        out_specs=pl.BlockSpec((length, projected.shape[1]), lambda i: (i, 0)),
        out_shape=jax.ShapeDtypeStruct(projected.shape, jnp.bfloat16),
        scratch_shapes=[pltpu.VMEM((length, length), jnp.float32)],
    )(projected, grad_context, log_totals, segment_ids[:, None, :], segment_ids[:, :, None])


def shards(
    block_input,
    output_cotangent,
    segment_ids,
    qkv_weight,
    proj_weight,
    up_weight,
    down_weight,
    norm_params,
    qkv_moments,
    proj_moments,
    up_moments,
    down_moments,
    norm_moments,
):
    tensor_count = lax.axis_size(TP)
    local_heads = HEADS // tensor_count
    token_count = block_input.shape[0]
    seq_count = token_count // SEQ
    scale = HD ** (-0.5)
    ring = (lax.axis_size(DP), lax.axis_index(DP))
    low = jnp.bfloat16
    qkv_rows = qkv_weight.reshape(qkv_weight.shape[0], -1)
    qkv_flat = gather_weight(qkv_rows.astype(low), False, ring)
    up_cols = up_weight.shape[1]
    up_proj = gather_weight(
        jnp.concatenate([up_weight, proj_weight], axis=1).astype(low), False, ring
    )
    up_full = up_proj[:, :up_cols]
    proj_full = up_proj[:, up_cols:]
    down_full = gather_weight(down_weight.astype(low), True, ring)
    gain_one, shift_one, gain_two, shift_two = (
        norm_params[0],
        norm_params[1],
        norm_params[2],
        norm_params[3],
    )
    normed_in, unit_one, inv_one = layer_norm(block_input, gain_one, shift_one)
    normed_low = normed_in.astype(jnp.bfloat16)
    projected = jnp.dot(normed_low, qkv_flat, preferred_element_type=jnp.float32).astype(
        jnp.bfloat16
    )
    per_seq = projected.reshape(seq_count, SEQ, 3, local_heads, HD)

    def scores_of(query_vals, key_vals, segment_row):
        scores = (
            jnp.einsum("qhd,khd->hqk", query_vals, key_vals, preferred_element_type=jnp.float32)
            * scale
        )
        return jnp.where(seq_mask(segment_row)[None], scores, masked_score)

    def attend(item):
        block, segment_row = item
        scores = scores_of(block[:, 0], block[:, 1], segment_row)
        top = jnp.max(scores, axis=-1, keepdims=True)
        log_total = top + jnp.log(jnp.sum(jnp.exp(scores - top), axis=-1, keepdims=True))
        probs = jnp.exp(scores - log_total).astype(jnp.bfloat16)
        context = jnp.einsum("hqk,khd->qhd", probs, block[:, 2], preferred_element_type=jnp.float32)
        return (context.astype(jnp.bfloat16), log_total)

    context_low, log_totals = lax.map(attend, (per_seq, segment_ids))
    context_flat = context_low.reshape(token_count, -1)
    attn_part = jnp.einsum("tc,ec->te", context_flat, proj_full, preferred_element_type=jnp.float32)
    mixed = block_input + sum_axis(attn_part, TP)
    normed_mid, unit_two, inv_two = layer_norm(mixed, gain_two, shift_two)
    mid_low = normed_mid.astype(jnp.bfloat16)
    pre_act = jnp.dot(mid_low, up_full, preferred_element_type=jnp.float32)
    act_low = gelu_tanh(pre_act).astype(jnp.bfloat16)
    mlp_part = jnp.einsum("tf,ef->te", act_low, down_full, preferred_element_type=jnp.float32)
    mlp_low = mlp_part.astype(low)
    mlp_other = exchange(mlp_low, TP, 0)
    block_output = mixed + (mlp_low.astype(jnp.float32) + mlp_other.astype(jnp.float32))
    grad_low = output_cotangent.astype(jnp.bfloat16)
    grad_act = jnp.dot(grad_low, down_full, preferred_element_type=jnp.float32)
    grad_pre = (grad_act * gelu_slope(pre_act)).astype(jnp.bfloat16)
    mid_part = jnp.einsum("tf,df->td", grad_pre, up_full, preferred_element_type=jnp.float32)
    grad_mid = sum_axis(mid_part, TP)
    grad_mixed = output_cotangent + norm_backward(grad_mid, unit_two, inv_two, gain_two)
    mixed_low = grad_mixed.astype(jnp.bfloat16)
    grad_context = jnp.dot(mixed_low, proj_full, preferred_element_type=jnp.float32).astype(
        jnp.bfloat16
    )

    grad_flat = attend_back(
        projected, grad_context, log_totals.reshape(seq_count, local_heads, SEQ), segment_ids
    )
    normed_part = jnp.einsum("tc,dc->td", grad_flat, qkv_flat, preferred_element_type=jnp.float32)
    grad_normed = sum_axis(normed_part, TP)
    input_grad = grad_mixed + norm_backward(grad_normed, unit_one, inv_one, gain_one)

    def weight_grad(tokens, grads, late):
        half = grads.shape[1] // 2
        left, right = (
            jnp.einsum("tr,tc->rc", tokens, part, preferred_element_type=jnp.float32)
            for part in (grads[:, :half], grads[:, half:])
        )
        return scatter_grad(left, right, late, ring)

    down_grad = weight_grad(grad_low, act_low, True)
    up_grad = weight_grad(mid_low, grad_pre, False)
    qkv_grad = weight_grad(normed_low, grad_flat, False).reshape(qkv_weight.shape)
    proj_grad = weight_grad(mixed_low, context_flat, False)
    share = token_count // tensor_count
    start = lax.axis_index(TP) * share
    grad_one = lax.dynamic_slice_in_dim(grad_normed, start, share, 0)
    unit_first = lax.dynamic_slice_in_dim(unit_one, start, share, 0)
    grad_two = lax.dynamic_slice_in_dim(grad_mid, start, share, 0)
    unit_second = lax.dynamic_slice_in_dim(unit_two, start, share, 0)
    norm_grad = jnp.stack(
        [
            jnp.sum(grad_one * unit_first, axis=0),
            jnp.sum(grad_one, axis=0),
            jnp.sum(grad_two * unit_second, axis=0),
            jnp.sum(grad_two, axis=0),
        ]
    )
    norm_grad = sum_axis(sum_axis(norm_grad, TP), DP)
    qkv_new, qkv_moments_new = adamw(qkv_weight, qkv_moments, qkv_grad, decay_rate)
    proj_new, proj_moments_new = adamw(proj_weight, proj_moments, proj_grad, decay_rate)
    up_new, up_moments_new = adamw(up_weight, up_moments, up_grad, decay_rate)
    down_new, down_moments_new = adamw(down_weight, down_moments, down_grad, decay_rate)
    norm_new, norm_moments_new = adamw(norm_params, norm_moments, norm_grad, 0.0)
    return (
        block_output,
        input_grad,
        qkv_grad,
        proj_grad,
        up_grad,
        down_grad,
        norm_grad,
        qkv_new,
        proj_new,
        up_new,
        down_new,
        norm_new,
        qkv_moments_new,
        proj_moments_new,
        up_moments_new,
        down_moments_new,
        norm_moments_new,
    )


def solution(mesh):
    in_specs = (
        P(DP, None),
        P(DP, None),
        P(DP, None),
        P(DP, None, TP),
        P(DP, TP),
        P(DP, TP),
        P(DP, TP),
        P(),
        P(None, DP, None, TP),
        P(None, DP, TP),
        P(None, DP, TP),
        P(None, DP, TP),
        P(),
    )
    out_specs = (
        P(DP, None),
        P(DP, None),
        P(DP, None, TP),
        P(DP, TP),
        P(DP, TP),
        P(DP, TP),
        P(),
        P(DP, None, TP),
        P(DP, TP),
        P(DP, TP),
        P(DP, TP),
        P(),
        P(None, DP, None, TP),
        P(None, DP, TP),
        P(None, DP, TP),
        P(None, DP, TP),
        P(),
    )

    return jax.shard_map(shards, mesh=mesh, in_specs=in_specs, out_specs=out_specs, check_vma=False)
```
